256 devices in a mesh: gx: 32 (over z, y_hi, core), gy: 8 (over x, y_lo).
Axes of the slice: x: 4, y: 4 (y_hi: 2, y_lo: 2; y = y_hi * 2 + y_lo), z: 8, core: 2. Of those that a mesh axis runs over, the one named last changes fastest.
Arguments:
- prior_members: float32 [64, 3, 2, 256, 1024], P(None, None, None, 'gx', 'gy'), may hold values from -0.25 to 0.25
- obs_column: int32 [32, 8, 256], P('gx', 'gy'), may hold values from 0 to 1023
- obs_value: float32 [32, 8, 256], P('gx', 'gy'), may hold values from -0.3 to 0.3
- obs_precision: float32 [32, 8, 256], P('gx', 'gy'), may hold values from 20 to 400
- obs_list: int32 [32, 128, 128], P('gx', 'gy'), may hold values from 0 to 2303, as said below
- patch_count: int32 [32, 128], P('gx', 'gy'), may hold values from 1 to 128, as said below
Outputs:
- analysis: float32 [64, 3, 2, 256, 1024], P(None, None, None, 'gx', 'gy')
The draws below stay inside these ranges and needn't reach their ends.
Inputs may be any that keep to these rules, and one draw needn't show every extreme that they name: `obs_list`: entry e of a patch's list names slot e % 256 of the tile displaced by (e // 256 // 3 - 1, e // 256 % 3 - 1) tiles in (longitude, latitude) from the patch's own tile, longitude wrapping around; never a tile beyond the latitude edges. Entries at and past the patch's count are ignored. `patch_count`: counts differ strongly from tile to tile.
All inputs are finite; a program needn't handle non-finite values.
Results may differ from the reference program's by a relative error of at most 0.0003.
Values sent between devices are 32-bit elements; how exact they have to be, the bound alone decides.
No kernel may reach another device: no remote copies, remote signals or barrier semaphores. Data moves between devices by JAX's collectives and lax.ppermute only.
A program may use at most 64 MiB of HBM per device.

```python
import math
import jax
import jax.numpy as jnp
from jax import lax

K = 64
LEV = 2
CX = 8
CY = 128
TILE_WIDTH_CELLS = 8
STEPS = 3
OBS_DEV = 256
OBSERVATION_CAP = 128
NS_ITERS = 3
TILES_X = 32
TILES_Y = 8
NX = 256
NY = 1024
PX = 32
PY = 128


def observation_plan(key):
    base_key = jax.random.fold_in(key, 417)
    subkeys = jax.random.split(base_key, 6)
    raw_counts = jax.random.randint(subkeys[0], (TILES_X, TILES_Y), 0, OBS_DEV + 1)
    tile_counts = jnp.maximum(1, raw_counts * raw_counts // OBS_DEV)
    busiest = jax.random.randint(subkeys[1], (), 0, TILES_X * TILES_Y)
    flat_counts = tile_counts.reshape(-1)
    flat_counts = jnp.where(jnp.arange(TILES_X * TILES_Y) == busiest, OBS_DEV, flat_counts)
    tile_counts = flat_counts.reshape(TILES_X, TILES_Y)
    per_row = CX // TILE_WIDTH_CELLS
    per_col = CY // TILE_WIDTH_CELLS
    home_x = jnp.arange(PX) // per_row
    home_y = jnp.arange(PY) // per_col
    own_counts = tile_counts[home_x[:, None], home_y[None, :]]
    nominal = jnp.maximum(1, OBSERVATION_CAP * own_counts // OBS_DEV)
    jitter = jax.random.randint(subkeys[2], (PX, PY), 0, 4)
    counts = jnp.maximum(1, nominal - jitter * nominal // 8)
    first_x = busiest // TILES_Y * per_row
    first_y = busiest % TILES_Y * per_col
    marked = (jnp.arange(PX)[:, None] == first_x) & (jnp.arange(PY)[None, :] == first_y)
    counts = jnp.where(marked, OBSERVATION_CAP, counts)
    shift_x = jax.random.randint(subkeys[3], (PX, PY, OBSERVATION_CAP), -1, 2)
    shift_y = jax.random.randint(subkeys[4], (PX, PY, OBSERVATION_CAP), -1, 2)
    target_y = home_y[None, :, None] + shift_y
    shift_y = jnp.where((target_y >= 0) & (target_y < TILES_Y), shift_y, 0)
    source_x = (home_x[:, None, None] + shift_x) % TILES_X
    source_y = home_y[None, :, None] + shift_y
    available = tile_counts[source_x, source_y]
    slot_index = jax.random.randint(subkeys[5], (PX, PY, OBSERVATION_CAP), 0, available)
    entries = ((shift_x + 1) * 3 + shift_y + 1) * OBS_DEV + slot_index
    return (counts.astype(jnp.int32), entries.astype(jnp.int32))


def draw_obs_list(key, part):
    return observation_plan(key)[1]


def draw_patch_count(key, part):
    return observation_plan(key)[0]


def plant(drawn, stream_key, smallest, largest):
    extent = drawn.shape
    index_at = [jax.random.randint(jax.random.fold_in(stream_key, axis), (), 0, extent[axis]) for axis in range(len(extent))]
    drawn = drawn.at[tuple(index_at)].set(smallest)
    longest = extent.index(max(extent))
    index_at[longest] = (index_at[longest] + 1) % extent[longest]
    return drawn.at[tuple(index_at)].set(largest)


def steps_of(own_key, dims, cuts, low, largest):
    def one(position, parts):
        steps = jax.random.uniform(jax.random.fold_in(jax.random.fold_in(own_key, 6), position), (parts,), jnp.float32, low / len(cuts), largest / len(cuts))
        return jnp.repeat(jnp.exp(steps), dims[position] // parts).reshape((-1,) + (1,) * (len(dims) - position - 1))

    gain = one(*cuts[0])
    for cut in cuts[1:]:
        gain = gain * one(*cut)
    return gain


def noise(rng, dims, width, most, cuts=(), held_as=jnp.bfloat16):
    drawn = width * jax.random.normal(rng, dims, jnp.float32)
    if cuts:
        drawn = drawn * steps_of(rng, dims, cuts, -0.22, 0.18)
    return jnp.clip(drawn, -most, most).astype(held_as)


def setup_inputs(seed: int = 0) -> dict:
    splits = jax.random.split(jax.random.key(seed), 7)
    return {
        "prior_members": jnp.clip(jax.random.uniform(splits[0], (K, 3, LEV, NX, NY), jnp.float32, -0.25, 0.25) * steps_of(splits[0], (K, 3, LEV, NX, NY), ((3, 32), (4, 8)), -0.4, 0.0), -0.25, 0.25),
        "obs_column": plant(jax.random.randint(splits[1], (TILES_X, TILES_Y, OBS_DEV), 0, CX * CY), jax.random.fold_in(splits[1], 1), 0, (CX * CY) - 1).astype(jnp.int32),
        "obs_value": noise(splits[2], (TILES_X, TILES_Y, OBS_DEV), 0.05, 0.3, ((0, 32), (1, 8)), jnp.float32),
        "obs_precision": jnp.clip(jnp.exp(math.log(400.0) - 2.9957323 * jax.random.uniform(splits[3], (TILES_X, TILES_Y, OBS_DEV), jnp.float32) ** steps_of(splits[3], (TILES_X, TILES_Y, OBS_DEV), ((0, 32), (1, 8)), -0.2, 0.2)), 20.0, 400.0),
        "obs_list": draw_obs_list(jax.random.fold_in(splits[6], 71), 0),
        "patch_count": draw_patch_count(jax.random.fold_in(splits[6], 71), 0),
    }


courant = 0.3
highest = lax.Precision.HIGHEST

def friedrichs_step(padded):
    depths = 1.0 + padded[..., 0, :, :, :]
    momentum_x = padded[..., 1, :, :, :]
    momentum_y = padded[..., 2, :, :, :]
    pressure = 0.5 * depths * depths
    cross_flux = momentum_x * momentum_y / depths
    flux_x = jnp.stack([momentum_x, momentum_x * momentum_x / depths + pressure, cross_flux], axis=-4)
    flux_y = jnp.stack([momentum_y, cross_flux, momentum_y * momentum_y / depths + pressure], axis=-4)
    neighbours = padded[..., 2:, 1:-1] + padded[..., :-2, 1:-1] + padded[..., 1:-1, 2:] + padded[..., 1:-1, :-2]
    return 0.25 * neighbours - 0.5 * courant * (flux_x[..., 2:, 1:-1] - flux_x[..., :-2, 1:-1]) - 0.5 * courant * (flux_y[..., 1:-1, 2:] - flux_y[..., 1:-1, :-2])

def analyse(fields, members_obs, values, precisions, offset_x, offset_y, usable):
    members = fields.shape[1]
    obs_mean = lax.optimization_barrier(jnp.mean(members_obs, axis=1))
    obs_pert = members_obs - obs_mean[:, None, :]
    departure = values - obs_mean
    weights = usable * precisions * jnp.exp(-(offset_x / CX) ** 2 - (offset_y / CY) ** 2)
    gram_matrix = jnp.einsum('bkm,bjm->bkj', obs_pert * weights[:, None, :], obs_pert, precision=highest)
    bounds = members - 1.0 + lax.optimization_barrier(jnp.sum(weights * lax.optimization_barrier(jnp.sum(obs_pert * obs_pert, axis=1)), axis=1))
    identity = jnp.eye(members, dtype=jnp.float32)
    scaled = (gram_matrix + (members - 1.0) * identity) / bounds[:, None, None]
    iterate = scaled
    inverse_root = jnp.broadcast_to(identity, scaled.shape)
    for repeat in range(NS_ITERS):
        factor = 1.5 * identity - 0.5 * jnp.einsum('bij,bjk->bik', inverse_root, iterate, precision=highest)
        iterate = jnp.einsum('bij,bjk->bik', iterate, factor, precision=highest)
        inverse_root = jnp.einsum('bij,bjk->bik', factor, inverse_root, precision=highest)
    forcing = jnp.einsum('bkm,bm->bk', obs_pert, weights * departure, precision=highest)
    half_way = jnp.einsum('bij,bj->bi', inverse_root, forcing, precision=highest)
    mean_weight = jnp.einsum('bij,bj->bi', inverse_root, half_way, precision=highest) / bounds[:, None]
    spread_weight = jnp.sqrt((members - 1.0) / bounds)[:, None, None] * inverse_root
    combined = spread_weight + mean_weight[:, :, None]
    field_mean = lax.optimization_barrier(jnp.mean(fields, axis=1))
    field_pert = fields - field_mean[:, None, :]
    return field_mean[:, None, :] + jnp.einsum('bif,bik->bkf', field_pert, combined, precision=highest)

def integrate_dynamics(states):
    for repeat in range(STEPS):
        wrapped = jnp.concatenate([states[..., -1:, :], states, states[..., :1, :]], axis=-2)
        padded = jnp.pad(wrapped, ((0, 0), (0, 0), (0, 0), (1, 1)))
        states = friedrichs_step(padded)
    return states

def reference(prior_members, obs_column, obs_value, obs_precision, obs_list, patch_count):
    predicted_fields = lax.map(integrate_dynamics, prior_members)
    layer_mean_value = lax.optimization_barrier(jnp.mean(predicted_fields[:, 0], axis=1))
    tile_x = jnp.arange(TILES_X, dtype=jnp.int32)[:, None, None]
    tile_y = jnp.arange(TILES_Y, dtype=jnp.int32)[None, :, None]
    local_x = obs_column // CY
    local_y = obs_column % CY
    members_obs = layer_mean_value[:, tile_x * CX + local_x, tile_y * CY + local_y]
    members_obs = jnp.transpose(members_obs, (1, 2, 0, 3))
    extras = jnp.stack([obs_value, obs_precision, local_x.astype(jnp.float32), local_y.astype(jnp.float32)], axis=2)
    obs_table = jnp.concatenate([members_obs, extras], axis=2)
    per_row = CX // TILE_WIDTH_CELLS
    per_col = CY // TILE_WIDTH_CELLS
    patch_y = jnp.arange(PY, dtype=jnp.int32)
    slot_range = jnp.arange(OBSERVATION_CAP, dtype=jnp.int32)

    def row_update(latitude_index):
        latitude_strip = lax.dynamic_slice_in_dim(predicted_fields, latitude_index * TILE_WIDTH_CELLS, TILE_WIDTH_CELLS, 3)
        blocks = latitude_strip.reshape(K, 3, LEV, TILE_WIDTH_CELLS, PY, TILE_WIDTH_CELLS)
        fields = jnp.transpose(blocks, (4, 0, 1, 2, 3, 5)).reshape(PY, K, 3 * LEV * TILE_WIDTH_CELLS * TILE_WIDTH_CELLS)
        entries = obs_list[latitude_index]
        offset = entries // OBS_DEV
        slot_index = entries % OBS_DEV
        shift_x = offset // 3 - 1
        shift_y = offset % 3 - 1
        home_x = latitude_index // per_row
        home_y = patch_y // per_col
        source_x = (home_x + shift_x) % TILES_X
        source_y = jnp.clip(home_y[:, None] + shift_y, 0, TILES_Y - 1)
        picked = obs_table[source_x, source_y, :, slot_index]
        picked_obs = jnp.transpose(picked[:, :, :K], (0, 2, 1))
        centre_x = (latitude_index % per_row * TILE_WIDTH_CELLS).astype(jnp.float32) + (TILE_WIDTH_CELLS - 1) * 0.5
        centre_y = (patch_y % per_col * TILE_WIDTH_CELLS).astype(jnp.float32) + (TILE_WIDTH_CELLS - 1) * 0.5
        offset_x = (shift_x * CX).astype(jnp.float32) + picked[:, :, K + 2] - centre_x
        offset_y = (shift_y * CY).astype(jnp.float32) + picked[:, :, K + 3] - centre_y[:, None]
        usable = (slot_range[None, :] < patch_count[latitude_index][:, None]).astype(jnp.float32)
        result = analyse(fields, picked_obs, picked[:, :, K], picked[:, :, K + 1], offset_x, offset_y, usable)
        result = result.reshape(PY, K, 3, LEV, TILE_WIDTH_CELLS, TILE_WIDTH_CELLS)
        return jnp.transpose(result, (1, 2, 3, 4, 0, 5)).reshape(K, 3, LEV, TILE_WIDTH_CELLS, NY)
    row_results = lax.map(row_update, jnp.arange(PX, dtype=jnp.int32))
    return jnp.transpose(row_results, (1, 2, 3, 0, 4, 5)).reshape(K, 3, LEV, NX, NY)
```

```python
import jax
import jax.numpy as jnp
from jax import lax
from jax.experimental import pallas as pl
from jax.experimental.pallas import tpu as pltpu
from jax.sharding import PartitionSpec as P

K = 64
CX = 8
CY = 128
W = 3
SLOTS = 256
CAP = 128
PATCHES = 16
PAIRS = 8
LATP = 160
LAT0 = 16
F32 = jnp.float32
BF = jnp.bfloat16
VM = pl.BlockSpec(memory_space=pltpu.VMEM)
SM = pl.BlockSpec(memory_space=pltpu.SMEM)
LIMIT = 60 * 1024 * 1024


def call(kernel, outs, ins, scratch=(), cost=None):
    return pl.pallas_call(
        kernel,
        out_shape=[jax.ShapeDtypeStruct(s, F32) for s in outs],
        in_specs=ins,
        out_specs=[VM] * len(outs),
        scratch_shapes=list(scratch),
        compiler_params=pltpu.CompilerParams(vmem_limit_bytes=LIMIT),
        cost_estimate=cost,
    )


def split(x):
    hi = x.astype(BF)
    return hi, (x - hi.astype(F32)).astype(BF)


def dot(a, b):
    return lax.dot_general(a, b, (((1,), (0,)), ((), ())), preferred_element_type=F32)


def dot_t(a, b):
    return lax.dot_general(a, b, (((1,), (1,)), ((), ())), preferred_element_type=F32)


def mm3(a, b, d=dot):
    return d(a[0], b[0]) + d(a[0], b[1]) + d(a[1], b[0])


def relayout(s_ref, x_ref, st_ref, t_ref, eoff_ref, eon_ref, ga_ref, gb_ref):
    px = s_ref[0]
    py = s_ref[1]
    for f in range(3):
        for lon in range(CX):
            low = x_ref[pl.ds(f * 16 + lon, K, stride=48), :]
            high = x_ref[pl.ds(f * 16 + 8 + lon, K, stride=48), :]
            t_ref[pl.ds((f * CX + lon) * CY, CY), :] = jnp.concatenate([low, high], axis=0).T
    start_off = jnp.where(px == 0, 0, CX - W)
    start_on = (CX - W) - start_off
    for f in range(3):
        for ref, start in ((eoff_ref, start_off), (eon_ref, start_on)):
            row = pl.multiple_of((f * CX + start) * CY, CY)
            ref[pl.ds(f * W * CY, W * CY), :] = t_ref[pl.ds(row, W * CY), :]
    for f in range(3):
        for la in range(W):
            south = t_ref[pl.ds(f * CX * CY + la, CX, stride=CY), :]
            north = t_ref[pl.ds(f * CX * CY + CY - W + la, CX, stride=CY), :]
            row = (f * W + la) * CX
            ga_ref[pl.ds(row, CX), :] = jnp.where(py == 0, north, south)
            gb_ref[pl.ds(row, CX), :] = jnp.where(py == 0, south, north)
    ga_ref[pl.ds(72, 8), :] = st_ref[...]
    gb_ref[pl.ds(72, 8), :] = st_ref[...]


def corners(s_ref, st_ref, ga_ref, gb_ref, coff_ref, con_ref):
    px = s_ref[0]
    for k, ref in enumerate((ga_ref, gb_ref)):
        for c in range(9):
            v = ref[pl.ds(c * CX, CX), :]
            lo = v[0:W]
            hi = v[CX - W : CX]
            row = (k * 9 + c) * W
            coff_ref[pl.ds(row, W), :] = jnp.where(px == 0, lo, hi)
            con_ref[pl.ds(row, W), :] = jnp.where(px == 0, hi, lo)
    pad = jnp.zeros((2, 128), F32)
    coff_ref[pl.ds(54, 2), :] = pad
    con_ref[pl.ds(54, 2), :] = pad
    for i, v in enumerate((st_ref[...], ga_ref[pl.ds(72, 8), :], gb_ref[pl.ds(72, 8), :])):
        coff_ref[pl.ds(56 + 8 * i, 8), :] = v
        con_ref[pl.ds(56 + 8 * i, 8), :] = v


def forecast(
    s_ref, col_ref, t_ref, roff_ref, ron_ref, ga_ref, gb_ref, coff_ref, con_ref,
    out_ref, obs_ref, q_ref, p_ref, bp_ref, bm_ref, tmp_ref,
):
    px = s_ref[0]
    py = s_ref[1]
    first = s_ref[2]
    last = s_ref[3]
    off_at = jnp.where(px == 0, 0, CX + W)
    on_at = (CX + W) - off_at
    NL = CX + 2 * W

    def base(f, lon):
        return (f * NL + lon) * LATP

    for f in range(3):
        for lon in range(CX):
            q_ref[pl.ds(base(f, lon + W) + LAT0, CY), :] = t_ref[pl.ds((f * CX + lon) * CY, CY), :]
        for ref, at in ((roff_ref, off_at), (ron_ref, on_at)):
            for i in range(W):
                row = pl.multiple_of(base(f, at + i) + LAT0, 8)
                q_ref[pl.ds(row, CY), :] = ref[pl.ds((f * W + i) * CY, CY), :]
    z5 = jnp.zeros((5, 128), F32)

    def put(f, lon, a, b):
        north = jnp.where(py == 0, a, b)
        south = jnp.where(py == 0, b, a)
        row = base(f, lon) + LAT0
        if not isinstance(row, int):
            row = pl.multiple_of(row, 8)
        q_ref[pl.ds(row - 8, 8), :] = jnp.concatenate([z5, south], axis=0)
        q_ref[pl.ds(row + CY, 8), :] = jnp.concatenate([north, z5], axis=0)

    for f in range(3):
        for lon in range(CX):
            a = ga_ref[pl.ds(f * W * CX + lon, W, stride=CX), :]
            b = gb_ref[pl.ds(f * W * CX + lon, W, stride=CX), :]
            put(f, lon + W, a, b)
        for ref, at in ((coff_ref, off_at), (con_ref, on_at)):
            for i in range(W):
                a = ref[pl.ds(f * 9 + i, W, stride=W), :]
                b = ref[pl.ds(27 + f * 9 + i, W, stride=W), :]
                put(f, at + i, a, b)

    for step in range(3):
        lo, hi = step, NL - 1 - step

        def flux(tile, carry):
            row = pl.multiple_of(tile * 8, 8)
            prev = []
            for lon in range(lo, hi + 1):
                hd = q_ref[pl.ds(base(0, lon) + row, 8), :]
                m = q_ref[pl.ds(base(1, lon) + row, 8), :]
                n = q_ref[pl.ds(base(2, lon) + row, 8), :]
                h = 1.0 + hd
                rh = 1.0 / h
                m5 = 0.15 * m
                n5 = 0.15 * n
                u5 = m5 * rh
                v5 = n5 * rh
                cross = u5 * n
                p5 = (0.075 * h) * h
                fm = u5 * m + p5
                gn = v5 * n + p5
                th, tm, tn = 0.25 * hd, 0.25 * m, 0.25 * n
                plus = (th + m5, tm + fm, tn + cross)
                minus = (th - m5, tm - fm, tn - cross)
                if lo < lon < hi:
                    for f, (t, g) in enumerate(((th, n5), (tm, cross), (tn, gn))):
                        bp_ref[pl.ds(base(f, lon) + row, 8), :] = t + g
                        bm_ref[pl.ds(base(f, lon) + row, 8), :] = t - g
                if len(prev) == 2:
                    for f in range(3):
                        p_ref[pl.ds(base(f, lon - 1) + row, 8), :] = prev[0][f] + minus[f]
                prev = (prev + [plus])[-2:]
            return carry

        lax.fori_loop(1, LATP // 8 - 1, flux, 0)
        final = step == 2

        def combine(tile, carry):
            row = pl.multiple_of(tile * 8, 8)
            outside = ((tile == 1) & (first == 1)) | ((tile == 18) & (last == 1))
            for lon in range(lo + 1, hi):
                for f in range(3):
                    at = base(f, lon) + row
                    v = (
                        p_ref[pl.ds(at, 8), :]
                        + bm_ref[pl.ds(at + 1, 8), :]
                        + bp_ref[pl.ds(at - 1, 8), :]
                    )
                    if final:
                        out_ref[pl.ds((f * CX + lon - W) * CY + row - LAT0, 8), :] = v
                    else:
                        q_ref[pl.ds(at, 8), :] = jnp.where(outside, 0.0, v)
            return carry

        if final:
            lax.fori_loop(2, 18, combine, 0)
        else:
            lax.fori_loop(1, 19, combine, 0)

    sub = lax.broadcasted_iota(jnp.int32, (8, 128), 0)
    lane = lax.broadcasted_iota(jnp.int32, (8, 128), 1)

    def rows8(start):
        v = jnp.broadcast_to(out_ref[pl.ds(col_ref[start], 1), :], (8, 128))
        for s in range(1, 8):
            w = jnp.broadcast_to(out_ref[pl.ds(col_ref[start + s], 1), :], (8, 128))
            v = jnp.where(sub == s, w, v)
        return 0.5 * (v + pltpu.roll(v, 64, 1))

    def pick(g, carry):
        left = rows8(g * 8)
        right = rows8(128 + g * 8)
        obs_ref[pl.ds(pl.multiple_of(g * 8, 8), 8), :] = jnp.where(lane < 64, left, right)
        return carry

    lax.fori_loop(0, 16, pick, 0)


def gather_pair(list_ref, tab_ref, y_ref, pair, groups):
    sub = lax.broadcasted_iota(jnp.int32, (8, 128), 0)
    left = lax.broadcasted_iota(jnp.int32, (8, 128), 1) < 64
    masks = [(sub == s) & left for s in range(8)] + [(sub == s) & (~left) for s in range(8)]

    def body(g, carry):
        at = pair * (2 * CAP) + g * 8
        v = None
        for half in range(2):
            for s in range(8):
                idx = list_ref[at + half * CAP + s]
                w = jnp.broadcast_to(tab_ref[pl.ds(idx, 1), :], (8, 128))
                v = w if v is None else jnp.where(masks[half * 8 + s], w, v)
        y_ref[pl.ds(pl.multiple_of(g * 8, 8), 8), :] = v
        return carry

    lax.fori_loop(0, groups, body, 0)


def tile_codes(px, py):
    dx_on = jnp.where(px == 0, 1, -1)
    dy_a = jnp.where(py == 0, 1, -1)
    return dx_on, dy_a


def weights(s_ref, cnt_ref, list_ref, st_ref, ga_ref, gb_ref, coff_ref, con_ref,
            r_ref, v_ref, tab_ref, y_ref):
    px = s_ref[0]
    py = s_ref[1]
    dx_on, dy_a = tile_codes(px, py)
    sources = [(st_ref[...], 0, 0), (ga_ref[pl.ds(72, 8), :], 0, dy_a), (gb_ref[pl.ds(72, 8), :], 0, -dy_a)]
    for ref, dx in ((coff_ref, -dx_on), (con_ref, dx_on)):
        for i, dy in enumerate((0, dy_a, -dy_a)):
            sources.append((ref[pl.ds(56 + 8 * i, 8), :], dx, dy))
    zero = jnp.zeros((61, 128), F32)
    for rows, dx, dy in sources:
        code = (dx + 1) * 3 + dy + 1
        fx = jnp.asarray(dx * CX, jnp.int32).astype(F32)
        fy = jnp.asarray(dy * CY, jnp.int32).astype(F32)
        value, prec, col = rows[0:2], rows[2:4], rows[4:6]
        lon = jnp.floor(col * (1.0 / CY))
        lat = col - lon * CY
        ox = (fx + lon - 3.5) * (1.0 / CX)
        wx = prec * jnp.exp(-(ox * ox))
        y = fy + lat
        for half in range(2):
            h = slice(half, half + 1)
            block = jnp.concatenate([wx[h], y[h], value[h], zero], axis=0)
            block = jnp.concatenate([block, block], axis=0)
            at = code * SLOTS + half * 128
            if not isinstance(at, int):
                at = pl.multiple_of(at, 128)
            tab_ref[pl.ds(at, 128), :] = block.T

    left = lax.broadcasted_iota(jnp.int32, (CAP, 128), 1) < 64
    entry = lax.broadcasted_iota(jnp.int32, (CAP, 128), 0)

    def body(pair, carry):
        gather_pair(list_ref, tab_ref, y_ref, pair, 16)
        g = y_ref[...]

        def both(i):
            a = jnp.broadcast_to(g[:, i : i + 1], (CAP, 128))
            b = jnp.broadcast_to(g[:, 64 + i : 65 + i], (CAP, 128))
            return jnp.where(left, a, b)

        centre = (pair * 16).astype(F32) + 3.5
        oy = (both(1) - jnp.where(left, centre, centre + 8.0)) * (1.0 / CY)
        count = jnp.where(left, cnt_ref[2 * pair], cnt_ref[2 * pair + 1])
        r = jnp.where(entry < count, both(0) * jnp.exp(-(oy * oy)), 0.0)
        at = pl.ds(pl.multiple_of(pair * CAP, CAP), CAP)
        r_ref[at, :] = r
        v_ref[at, :] = both(2)
        return carry

    lax.fori_loop(0, PAIRS, body, 0)


def analysis(
    s_ref, cnt_ref, list_ref, r_ref, v_ref, own_ref, oa_ref, ob_ref, on_ref, off_ref, fa_ref, fb_ref,
    t_ref, out_ref, tab_ref, y_ref, a_ref, z_ref, ya_ref, f_ref, c_ref, m_ref, o_ref,
):
    px = s_ref[0]
    py = s_ref[1]
    dx_on, dy_a = tile_codes(px, py)
    lane8 = lax.broadcasted_iota(jnp.int32, (128, 128), 1) < 64

    def unpack(packed, dx, dy):
        rolled = pltpu.roll(packed, 64, 1)
        at = pl.multiple_of(((dx + 1) * 3 + dy + 1) * SLOTS, SLOTS)
        tab_ref[pl.ds(at, 128), :] = jnp.where(lane8, packed, rolled)
        tab_ref[pl.ds(at + 128, 128), :] = jnp.where(lane8, rolled, packed)

    zero = jnp.int32(0)
    unpack(own_ref[...], zero, zero)
    unpack(oa_ref[...], zero, dy_a)
    unpack(ob_ref[...], zero, -dy_a)
    for i, dy in enumerate((zero, dy_a, -dy_a)):
        unpack(on_ref[pl.ds(i * 128, 128), :], dx_on, dy)
    unpack(off_ref[...], -dx_on, zero)
    unpack(fa_ref[...], -dx_on, dy_a)
    unpack(fb_ref[...], -dx_on, -dy_a)

    row = lax.broadcasted_iota(jnp.int32, (128, 128), 0)
    lane = lax.broadcasted_iota(jnp.int32, (128, 128), 1)
    same = (row < 64) == (lane < 64)
    eye = jnp.where(row == lane, 1.0, 0.0).astype(F32)
    mean_of = jnp.where(same, 1.0 / 64, 0.0).astype(BF)
    lane1 = lax.broadcasted_iota(jnp.int32, (1, 128), 1)
    y_ref[...] = jnp.zeros_like(y_ref)

    def gram(pair, carry):
        most = jnp.maximum(cnt_ref[2 * pair], cnt_ref[2 * pair + 1])
        gather_pair(list_ref, tab_ref, y_ref, pair, (most + 7) // 8)
        at = pl.ds(pl.multiple_of(pair * CAP, CAP), CAP)
        y = y_ref[...]
        yh, yl = split(y)
        mean = dot(yh, mean_of) + dot(yl, mean_of)
        pert = y - mean
        r = r_ref[at, :]
        rp = r * pert
        force = jnp.sum(rp * (v_ref[at, :] - mean), axis=0, keepdims=True)
        rt = split(rp.T)
        g = mm3(rt, split(pert))
        diag = jnp.sum(g * eye, axis=0, keepdims=True)
        ca = 63.0 + jnp.sum(jnp.where(lane1 < 64, diag, 0.0), axis=1, keepdims=True)
        cb = 63.0 + jnp.sum(jnp.where(lane1 < 64, 0.0, diag), axis=1, keepdims=True)
        c = jnp.where(lane1 < 64, ca, cb)
        a_ref[at, :] = jnp.where(same, (g + 63.0 * eye) / c, 0.0)
        f_ref[pl.ds(pair, 1), :] = force
        c_ref[pl.ds(pair, 1), :] = c
        return carry

    lax.fori_loop(0, PAIRS, gram, 0)

    def at(p):
        return pl.ds(p * CAP, CAP)

    pairs = range(PAIRS)
    for p in pairs:
        a = a_ref[at(p), :]
        s = 1.5 * eye - 0.5 * a
        z_ref[at(p), :] = s
        ya_ref[at(p), :] = mm3(split(a), split(s))
    for p in pairs:
        z = split(z_ref[at(p), :])
        y = split(ya_ref[at(p), :])
        a_ref[at(p), :] = 1.5 * eye - 0.5 * mm3(z, y)
    for p in pairs:
        s = split(a_ref[at(p), :])
        z = split(z_ref[at(p), :])
        y = split(ya_ref[at(p), :])
        z_ref[at(p), :] = mm3(s, z)
        ya_ref[at(p), :] = mm3(s, y)
    for p in pairs:
        z = split(z_ref[at(p), :])
        y = split(ya_ref[at(p), :])
        a_ref[at(p), :] = 1.5 * eye - 0.5 * mm3(z, y)
    for p in pairs:
        s = split(a_ref[at(p), :])
        z = split(z_ref[at(p), :])
        z = mm3(s, z)
        c = c_ref[pl.ds(p, 1), :]
        g = jnp.sum(z * f_ref[pl.ds(p, 1), :], axis=1, keepdims=True)
        wbar = jnp.sum(z * g, axis=0, keepdims=True) / c
        wt = z * jnp.sqrt(63.0 / c) + wbar
        wt = jnp.where(same, wt, 0.0)
        mean = jnp.sum(wt, axis=1, keepdims=True) * (1.0 / 64)
        m = jnp.where(same, wt + (1.0 / 64) - mean, 0.0)
        ma, mb = m[0:64], m[64:128]
        m_ref[pl.ds(2 * p * 128, 64), :] = ma
        m_ref[pl.ds(2 * p * 128 + 64, 64), :] = pltpu.roll(ma, 64, 1)
        m_ref[pl.ds((2 * p + 1) * 128, 64), :] = pltpu.roll(mb, 64, 1)
        m_ref[pl.ds((2 * p + 1) * 128 + 64, 64), :] = mb

    def update(p, carry):
        m = split(m_ref[pl.ds(pl.multiple_of(p * 128, 128), 128), :])
        rows = [t_ref[pl.ds(pl.multiple_of(i * CY + p * 8, 8), 8), :] for i in range(24)]
        x = split(jnp.concatenate(rows, axis=0))
        o = mm3(x, m, dot_t)
        for i in range(24):
            o_ref[pl.ds(pl.multiple_of(i * CY + p * 8, 8), 8), :] = o[i * 8 : i * 8 + 8]
        return carry

    lax.fori_loop(0, PATCHES, update, 0)
    for f in range(3):
        for lon in range(CX):
            v = o_ref[pl.ds((f * CX + lon) * CY, CY), :].T
            out_ref[pl.ds(f * 16 + lon, K, stride=48), :] = v[0:64]
            out_ref[pl.ds(f * 16 + 8 + lon, K, stride=48), :] = v[64:128]


def swaps(size, odd, ring):
    pairs = []
    for i in range(odd, size, 2):
        j = i + 1
        if j >= size:
            if not ring:
                continue
            j %= size
        pairs += [(i, j), (j, i)]
    return pairs


def local(prior_members, obs_column, obs_value, obs_precision, obs_list, patch_count):
    gx, gy = lax.axis_index("gx"), lax.axis_index("gy")
    nx, ny = lax.axis_size("gx"), lax.axis_size("gy")
    scalars = jnp.stack(
        [gx % 2, gy % 2, (gy == 0).astype(jnp.int32), (gy == ny - 1).astype(jnp.int32)]
    ).astype(jnp.int32)

    def on(x):
        return lax.ppermute(x, "gx", swaps(nx, 0, True))

    def off(x):
        return lax.ppermute(x, "gx", swaps(nx, 1, True))

    def gya(x):
        return lax.ppermute(x, "gy", swaps(ny, 0, False))

    def gyb(x):
        return lax.ppermute(x, "gy", swaps(ny, 1, False))

    columns = obs_column[0, 0]
    static = jnp.concatenate(
        [
            obs_value.reshape(2, 128),
            obs_precision.reshape(2, 128),
            columns.astype(F32).reshape(2, 128),
            jnp.zeros((2, 128), F32),
        ],
        axis=0,
    )
    entries = obs_list.reshape(PATCHES * CAP)
    counts = patch_count.reshape(PATCHES)
    x = prior_members.reshape(3072, 128)
    t, eoff, eon, ga, gb = call(
        relayout,
        [(3072, 128), (1152, 128), (1152, 128), (80, 128), (80, 128)],
        [SM, VM, VM],
    )(scalars, x, static)
    roff = off(eoff)
    ra = gya(ga)
    rb = gyb(gb)
    ron = on(eon)
    coff, con = call(corners, [(80, 128), (80, 128)], [SM, VM, VM, VM])(scalars, static, ra, rb)
    rcoff = off(coff)
    rcon = on(con)
    cells = 3 * 14 * LATP
    state, obs = call(
        forecast,
        [(3072, 128), (128, 128)],
        [SM, SM] + [VM] * 7,
        [pltpu.VMEM((cells, 128), F32)] * 4 + [pltpu.VMEM((8, 128), F32)],
    )(scalars, columns, t, roff, ron, ra, rb, rcoff, rcon)
    r, v = call(
        weights,
        [(1024, 128), (1024, 128)],
        [SM, SM, SM] + [VM] * 5,
        [pltpu.VMEM((9 * SLOTS, 128), F32), pltpu.VMEM((CAP, 128), F32)],
    )(scalars, counts, entries, static, ra, rb, rcoff, rcon)
    o_off = off(obs)
    o_a = gya(obs)
    o_b = gyb(obs)
    o_on = on(jnp.concatenate([obs, o_a, o_b], axis=0))
    f_a = gya(o_off)
    f_b = gyb(o_off)
    sq = pltpu.VMEM((1024, 128), F32)
    small = pltpu.VMEM((8, 128), F32)
    (out,) = call(
        analysis,
        [(3072, 128)],
        [SM, SM, SM] + [VM] * 10,
        [
            pltpu.VMEM((9 * SLOTS, 128), F32),
            pltpu.VMEM((CAP, 128), F32),
            sq,
            sq,
            sq,
            small,
            small,
            pltpu.VMEM((2048, 128), F32),
            pltpu.VMEM((3072, 128), F32),
        ],
    )(scalars, counts, entries, r, v, obs, o_a, o_b, o_on, o_off, f_a, f_b, state)
    return out.reshape(prior_members.shape)


def solution(mesh):
    return jax.shard_map(
        local,
        mesh=mesh,
        in_specs=(
            P(None, None, None, "gx", "gy"),
            P("gx", "gy", None),
            P("gx", "gy", None),
            P("gx", "gy", None),
            P("gx", "gy", None),
            P("gx", "gy"),
        ),
        out_specs=P(None, None, None, "gx", "gy"),
        check_vma=False,
    )
```
